32 devices in a mesh: sx: 4 (over z), sy: 4 (over y, x), dp: 2 (over core).
Axes of the slice: x: 2, y: 2, z: 4, core: 2. Of those that a mesh axis runs over, the one named last changes fastest.
Arguments:
- features: bfloat16 [2, 32, 32, 4, 8, 128], P('dp', 'sx', 'sy'), may hold values from -6 to 6
- cotangent: bfloat16 [2, 32, 32, 4, 8, 128], P('dp', 'sx', 'sy'), may hold values from -6 to 6
- first_weight: bfloat16 [27, 128, 128], replicated, may hold values from -0.109375 to 0.109375
- second_weight: bfloat16 [27, 128, 128], replicated, may hold values from -0.109375 to 0.109375
- neighbours: int32 [2, 4, 4, 4, 26], P('dp', 'sx', 'sy'), may hold values from -1 to 3, as said below
- counts: int32 [2, 4, 4], P('dp', 'sx', 'sy'), may hold values from 1 to 4, as said below
Outputs:
- out_field: bfloat16 [2, 32, 32, 4, 8, 128], P('dp', 'sx', 'sy')
- grad_input: bfloat16 [2, 32, 32, 4, 8, 128], P('dp', 'sx', 'sy')
- grad_first: float32 [27, 128, 128], replicated
- grad_second: float32 [27, 128, 128], replicated
The draws below stay inside these ranges and needn't reach their ends.
Inputs may be any that keep to these rules, and one draw needn't show every extreme that they name: Entries name only live slots; slots at or above a column's count have no neighbours; the relation is symmetric: if slot s of column (i, j) names slot t in direction d, then slot t of column (i+dx, j+dy) names s in the opposite direction, and the blocks are adjacent in space; columns outside the grid are never named. `counts`: some column of every workpiece has 4 live slots.
All inputs are finite; a program needn't handle non-finite values.
Results may differ from the reference program's by a relative error of at most 0.012.
Values may be sent and summed in bfloat16 or wider, within the bound.
A program may use at most 192 MiB of HBM per device.

```python
import jax
import jax.numpy as jnp
from jax import lax

C = 128
BE = 8
NB = 4
BATCH = 2
COLS_X = 4
COLS_Y = 4
XV = 32
YV = 32


def column_layout(key):
    height_key = jax.random.fold_in(key, 7)
    count_key = jax.random.fold_in(key, 11)
    chosen_key = jax.random.fold_in(key, 13)
    heights = jax.random.randint(height_key, (BATCH, COLS_X, COLS_Y), 0, 2)
    drawn = jax.random.randint(count_key, (BATCH, COLS_X * COLS_Y), 1, NB + 1)
    chosen = jax.random.randint(chosen_key, (BATCH,), 0, COLS_X * COLS_Y)
    forced = jnp.arange(COLS_X * COLS_Y)[None, :] == chosen[:, None]
    counts = jnp.where(forced, NB, drawn).reshape(BATCH, COLS_X, COLS_Y)
    return (heights.astype(jnp.int32), counts.astype(jnp.int32))


def draw_counts(key, part):
    heights, counts = column_layout(key)
    return counts


def draw_neighbours(key, part):
    heights, counts = column_layout(key)
    slot_ids = jnp.arange(NB, dtype=jnp.int32)
    height_pad = jnp.pad(heights, ((0, 0), (1, 1), (1, 1)))
    count_pad = jnp.pad(counts, ((0, 0), (1, 1), (1, 1)))
    entries = []
    for shift_x in range(3):
        for shift_y in range(3):
            for shift_z in range(3):
                if shift_x * 9 + shift_y * 3 + shift_z == 13:
                    continue
                near_height = height_pad[:, shift_x:shift_x + COLS_X, shift_y:shift_y + COLS_Y]
                near_count = count_pad[:, shift_x:shift_x + COLS_X, shift_y:shift_y + COLS_Y]
                target = heights[..., None] + slot_ids + (shift_z - 1) - near_height[..., None]
                valid = (target >= 0) & (target < near_count[..., None]) & (slot_ids < counts[..., None])
                entries.append(jnp.where(valid, target, -1))
    return jnp.stack(entries, axis=-1).astype(jnp.int32)


def shard_levels(rng, extent, cuts, least, top_value):
    def one(axis_at, parts):
        steps = jax.random.uniform(jax.random.fold_in(jax.random.fold_in(rng, 6), axis_at), (parts,), jnp.float32, least / len(cuts), top_value / len(cuts))
        return jnp.repeat(jnp.exp(steps), extent[axis_at] // parts).reshape((-1,) + (1,) * (len(extent) - axis_at - 1))

    level = one(*cuts[0])
    for cut in cuts[1:]:
        level = level * one(*cut)
    return level


def normal_values(key, shape, scale, limit, split=(), kind=jnp.bfloat16):
    gain = shard_levels(key, shape, split, -0.22, 0.18) if split else 1.0
    values = jax.random.normal(key, shape, jnp.float32) * scale * gain
    return jnp.minimum(jnp.maximum(values, -limit), limit).astype(kind)


def setup_inputs(seed: int = 0) -> dict:
    streams_of = jax.random.split(jax.random.key(seed), 7)
    return {
        "features": normal_values(streams_of[0], (BATCH, XV, YV, NB, BE, C), 1.0, 6.0, ((0, 2), (1, 4), (2, 4))),
        "cotangent": normal_values(streams_of[1], (BATCH, XV, YV, NB, BE, C), 1.0, 6.0, ((0, 2), (1, 4), (2, 4))),
        "first_weight": normal_values(streams_of[2], (27, C, C), (27 * C) ** -0.5, 0.109375),
        "second_weight": normal_values(streams_of[3], (27, C, C), (27 * C) ** -0.5, 0.109375),
        "neighbours": draw_neighbours(jax.random.fold_in(streams_of[6], 71), 0),
        "counts": draw_counts(jax.random.fold_in(streams_of[6], 71), 0),
    }


def padded_blocks(halo_field, neighbour):
    block_edge = halo_field.shape[0] - 2
    ranges_xy = [(0, 1), (1, block_edge + 1), (block_edge + 1, block_edge + 2)]
    ranges_z = [(block_edge - 1, block_edge), (0, block_edge), (0, 1)]
    planes = []
    for shift_x in range(3):
        row_list = []
        for shift_y in range(3):
            slab_list = []
            for shift_z in range(3):
                direction = shift_x * 9 + shift_y * 3 + shift_z
                low_x, high_x = ranges_xy[shift_x]
                low_y, high_y = ranges_xy[shift_y]
                low_z, high_z = ranges_z[shift_z]
                region = halo_field[low_x:high_x, low_y:high_y, :, low_z:high_z]
                if direction == 13:
                    slab_piece = region
                else:
                    entry = direction if direction < 13 else direction - 1
                    target = neighbour[:, entry]
                    valid = (target >= 0).astype(region.dtype)[None, None, :, None, None]
                    slab_piece = jnp.take(region, jnp.maximum(target, 0), axis=2) * valid
                slab_list.append(slab_piece)
            row_list.append(jnp.concatenate(slab_list, axis=3))
        planes.append(jnp.concatenate(row_list, axis=1))
    return jnp.concatenate(planes, axis=0)


def patch_matrix(padded, block_edge):
    pieces = []
    for shift_x in range(3):
        for shift_y in range(3):
            for shift_z in range(3):
                pieces.append(padded[shift_x:shift_x + block_edge, shift_y:shift_y + block_edge, :, shift_z:shift_z + block_edge])
    stacked = jnp.concatenate(pieces, axis=-1)
    return stacked.reshape(-1, stacked.shape[-1])


def flipped_weight(weight):
    return jnp.transpose(weight[::-1], (0, 2, 1))


def silu_slope(values):
    logistic = jax.nn.sigmoid(values)
    return logistic * (1.0 + values * (1.0 - logistic))


def column_start(column_x, column_y):
    zero_index = jnp.zeros((), jnp.int32)
    start_x = (column_x * BE).astype(jnp.int32)
    start_y = (column_y * BE).astype(jnp.int32)
    return (start_x, start_y, zero_index, zero_index, zero_index)


def column_patches(padded_field, neighbours_w, column_id):
    column_x = (column_id // COLS_Y).astype(jnp.int32)
    column_y = (column_id % COLS_Y).astype(jnp.int32)
    halo_field = lax.dynamic_slice(padded_field, column_start(column_x, column_y), (BE + 2, BE + 2, NB, BE, C))
    return patch_matrix(padded_blocks(halo_field, neighbours_w[column_x, column_y]), BE)


def pad_field(field):
    return jnp.pad(field, ((1, 1), (1, 1), (0, 0), (0, 0), (0, 0)))


def convolve_field(field, neighbours_w, weight):
    padded_field = pad_field(field)
    matrix = weight.reshape(27 * C, C)

    def per_column(column_id):
        columns = column_patches(padded_field, neighbours_w, column_id)
        return jnp.dot(columns, matrix, preferred_element_type=jnp.float32).reshape(BE, BE, NB, BE, C)

    result = lax.map(per_column, jnp.arange(COLS_X * COLS_Y, dtype=jnp.int32))
    result = result.reshape(COLS_X, COLS_Y, BE, BE, NB, BE, C)
    return jnp.transpose(result, (0, 2, 1, 3, 4, 5, 6)).reshape(XV, YV, NB, BE, C)


def weight_grad_field(field, grad_field, neighbours_w):
    padded_field = pad_field(field)

    def advance(running, column_id):
        columns = column_patches(padded_field, neighbours_w, column_id)
        column_x = (column_id // COLS_Y).astype(jnp.int32)
        column_y = (column_id % COLS_Y).astype(jnp.int32)
        grads = lax.dynamic_slice(grad_field, column_start(column_x, column_y), (BE, BE, NB, BE, C)).reshape(-1, C)
        term = lax.dot_general(columns, grads, (((0,), (0,)), ((), ())), preferred_element_type=jnp.float32)
        return running + term, None

    running, unused = lax.scan(advance, jnp.zeros((27 * C, C), jnp.float32), jnp.arange(COLS_X * COLS_Y, dtype=jnp.int32))
    return running.reshape(27, C, C)


def live_field(counts_w):
    live_mask = (jnp.arange(NB, dtype=jnp.int32)[None, None, :] < counts_w[:, :, None]).astype(jnp.float32)
    live_mask = jnp.repeat(jnp.repeat(live_mask, BE, axis=0), BE, axis=1)
    return live_mask[:, :, :, None, None]


def reference(features, cotangent, first_weight, second_weight, neighbours, counts):
    grad_scale = float(BATCH * COLS_X * COLS_Y * NB * BE ** 3) ** -0.5
    flip_first = flipped_weight(first_weight)
    flip_second = flipped_weight(second_weight)
    outputs = []
    input_grads = []
    first_total = jnp.zeros((27, C, C), jnp.float32)
    second_total = jnp.zeros((27, C, C), jnp.float32)
    for member in range(BATCH):
        live_mask = live_field(counts[member])
        links = neighbours[member]
        masked = features[member] * live_mask.astype(features.dtype)
        pre_first = convolve_field(masked, links, first_weight)
        hidden = (jax.nn.silu(pre_first) * live_mask).astype(jnp.bfloat16)
        pre_second = convolve_field(hidden, links, second_weight)
        summed = masked.astype(jnp.float32) + pre_second
        outputs.append((jax.nn.silu(summed) * live_mask).astype(jnp.bfloat16))
        back_second = (cotangent[member].astype(jnp.float32) * silu_slope(summed) * live_mask).astype(jnp.bfloat16)
        second_total = second_total + weight_grad_field(hidden, back_second, links)
        back_hidden = convolve_field(back_second, links, flip_second)
        back_first = (back_hidden * silu_slope(pre_first) * live_mask).astype(jnp.bfloat16)
        first_total = first_total + weight_grad_field(masked, back_first, links)
        back_input = convolve_field(back_first, links, flip_first)
        input_grads.append(((back_second.astype(jnp.float32) + back_input) * live_mask).astype(jnp.bfloat16))
    return (jnp.stack(outputs), jnp.stack(input_grads), first_total * grad_scale, second_total * grad_scale)
```

```python
import functools

import jax
import jax.numpy as jnp
from jax import lax
from jax.experimental import pallas as pl
from jax.experimental.pallas import tpu as pltpu
from jax.sharding import PartitionSpec as P

DIRS = [(dx, dy) for dx in (-1, 0, 1) for dy in (-1, 0, 1) if (dx, dy) != (0, 0)]
F32 = jnp.float32
BF16 = jnp.bfloat16


def slope(v):
    s = jax.nn.sigmoid(v)
    return s * (1.0 + v * (1.0 - s))


def kernel(
    nx,
    ny,
    feat,
    cot,
    w1,
    w2,
    w1f,
    w2f,
    sel,
    live,
    out_ref,
    gin_ref,
    gw1_ref,
    gw2_ref,
    fld,
    rx,
    ry,
    rc,
    pc_a,
    pc_b,
    pc_c,
    pre,
    gt,
    send_sem,
    recv_sem,
):
    edge = feat.shape[0]
    rows = feat.shape[2]
    ch = feat.shape[3]
    pairs = edge // 2
    plane = edge * rows
    ix = lax.axis_index("sx")
    iy = lax.axis_index("sy")

    def there(dx, dy):
        ok = None
        for d, i, n in ((dx, ix, nx), (dy, iy, ny)):
            if d == 0:
                continue
            c = (i < n - 1) if d > 0 else (i > 0)
            ok = c if ok is None else jnp.logical_and(ok, c)
        return ok

    def peer(dx, dy):
        px = jnp.minimum(jnp.maximum(ix + dx, 0), nx - 1)
        py = jnp.minimum(jnp.maximum(iy + dy, 0), ny - 1)
        return {"sx": px, "sy": py}

    def halo_ref(f, dx, dy):
        if dy == 0:
            return rx.at[f, (dx + 1) // 2]
        if dx == 0:
            return ry.at[f, (dy + 1) // 2]
        return rc.at[f, (dx + 1) // 2 * 2 + (dy + 1) // 2]

    def desc(f, k):
        dx, dy = DIRS[k]
        far_x = edge - 1 if dx > 0 else 0
        far_y = edge - 1 if dy > 0 else 0
        if dy == 0:
            src = fld.at[f, far_x]
        elif dx == 0:
            src = fld.at[f, :, far_y]
        else:
            src = fld.at[f, far_x, far_y]
        return pltpu.make_async_remote_copy(
            src_ref=src,
            dst_ref=halo_ref(f, -dx, -dy),
            send_sem=send_sem.at[f, k],
            recv_sem=recv_sem.at[f, k],
            device_id=peer(dx, dy),
            device_id_type=pl.DeviceIdType.MESH,
        )

    def send(f):
        for k, (dx, dy) in enumerate(DIRS):
            @pl.when(there(dx, dy))
            def _(k=k):
                desc(f, k).start()

    def arrive(f):
        for k, (dx, dy) in enumerate(DIRS):
            @pl.when(there(-dx, -dy))
            def _(k=k):
                desc(f, k).wait_recv()

    def drain(f):
        for k, (dx, dy) in enumerate(DIRS):
            @pl.when(there(dx, dy))
            def _(k=k):
                desc(f, k).wait_send()

    def put(pc, x, yp, tile):
        t = tile.astype(BF16)
        for b in range(3):
            y = yp - b
            if 0 <= y < edge:
                for c in range(3):
                    lo = (b * 3 + c) * ch
                    pc[x, y, :, lo : lo + ch] = t[c * rows : (c + 1) * rows]

    def line(pc, x, s, tiles):
        cat = jnp.concatenate(tiles, axis=1)
        got = jnp.dot(s, cat, preferred_element_type=F32)
        for y in range(edge):
            put(pc, x, y + 1, got[:, y * ch : (y + 1) * ch])

    def inner(f, pc):
        def body(x, carry):
            line(pc, x + 1, sel[4], [fld[f, x, y] for y in range(edge)])
            return carry

        lax.fori_loop(0, edge, body, 0)

    def outer(f, pc):
        for h in range(2):
            x = 0 if h == 0 else edge + 1
            line(pc, x, sel[6 * h + 1], [rx[f, h, y] for y in range(edge)])
            for g in range(2):
                yp = 0 if g == 0 else edge + 1
                put(pc, x, yp, jnp.dot(sel[6 * h + 2 * g], rc[f, h * 2 + g], preferred_element_type=F32))
            cat = jnp.concatenate([ry[f, h, x] for x in range(edge)], axis=1)
            got = jnp.dot(sel[3 + 2 * h], cat, preferred_element_type=F32)
            for x in range(edge):
                put(pc, x + 1, 0 if h == 0 else edge + 1, got[:, x * ch : (x + 1) * ch])

    def conv(pc, w, use):
        def body(i, carry):
            left = None
            right = None
            for p in range(4):
                lhs = pc[2 * i + p].reshape(plane, 9 * ch)
                wl = w[p] if p < 3 else None
                wr = w[p - 1] if p > 0 else None
                if wr is None:
                    left = jnp.dot(lhs, wl, preferred_element_type=F32)
                elif wl is None:
                    right = right + jnp.dot(lhs, wr, preferred_element_type=F32)
                else:
                    both = jnp.dot(lhs, jnp.concatenate([wl, wr], axis=1), preferred_element_type=F32)
                    left = left + both[:, :ch]
                    right = both[:, ch:] if right is None else right + both[:, ch:]
            use(i, 0, left)
            use(i, 1, right)
            return carry

        lax.fori_loop(0, pairs, body, 0)

    def keep_t(i, h, v):
        gt[h * ch : (h + 1) * ch, pl.ds(pl.multiple_of(i * plane, plane), plane)] = v.T.astype(BF16)

    def wgrad(pc, gw):
        def body(b, carry):
            for p in range(4):
                lanes = pl.ds(pl.multiple_of(b * (3 * ch), 3 * ch), 3 * ch)
                acc = None
                for i in range(pairs):
                    rhs = pc[2 * i + p, :, :, lanes].reshape(plane, 3 * ch)
                    lhs = gt[:, i * plane : (i + 1) * plane]
                    if p == 0:
                        lhs = lhs[:ch]
                    elif p == 3:
                        lhs = lhs[ch:]
                    t = jnp.dot(lhs, rhs, preferred_element_type=F32)
                    acc = t if acc is None else acc + t
                if p == 0:
                    gw[0, b] = acc
                elif p == 3:
                    gw[2, b] = gw[2, b] + acc
                else:
                    gw[p - 1, b] = gw[p - 1, b] + acc[ch:]
                    gw[p, b] = acc[:ch]
            return carry

        lax.fori_loop(0, 3, body, 0)

    for dx, dy in DIRS:
        @pl.when(jnp.logical_not(there(dx, dy)))
        def _(dx=dx, dy=dy):
            for f in range(4):
                r = halo_ref(f, dx, dy)
                r[...] = jnp.zeros(r.shape, BF16)

    barrier = pltpu.get_barrier_semaphore()
    for dx, dy in DIRS:
        @pl.when(there(dx, dy))
        def _(dx=dx, dy=dy):
            pl.semaphore_signal(barrier, inc=1, device_id=peer(dx, dy), device_id_type=pl.DeviceIdType.MESH)

    def mask_in(x, carry):
        v = feat[x].astype(F32).reshape(plane, ch) * live[...]
        fld[0, x] = v.astype(BF16).reshape(edge, rows, ch)
        return carry

    lax.fori_loop(0, edge, mask_in, 0)

    near_x = jnp.minimum(ix, 1) + jnp.minimum(nx - 1 - ix, 1) + 1
    near_y = jnp.minimum(iy, 1) + jnp.minimum(ny - 1 - iy, 1) + 1
    pl.semaphore_wait(barrier, near_x * near_y - 1)

    def store(f, x, v):
        fld[f, x] = v.astype(BF16).reshape(edge, rows, ch)

    send(0)
    inner(0, pc_a)
    arrive(0)
    outer(0, pc_a)

    def use1(i, h, v):
        x = 2 * i + h
        pre[x] = v
        store(1, x, v * jax.nn.sigmoid(v) * live[...])

    conv(pc_a, w1, use1)
    send(1)
    inner(1, pc_b)
    arrive(1)
    outer(1, pc_b)

    def use2(i, h, v):
        x = 2 * i + h
        v = v + fld[0, x].reshape(plane, ch).astype(F32)
        s = jax.nn.sigmoid(v)
        out_ref[x] = (v * s * live[...]).astype(BF16).reshape(edge, rows, ch)
        g = cot[x].reshape(plane, ch).astype(F32) * (s * (1.0 + v * (1.0 - s))) * live[...]
        store(2, x, g)
        keep_t(i, h, g)

    conv(pc_b, w2, use2)
    send(2)
    inner(2, pc_c)
    wgrad(pc_b, gw2_ref)
    arrive(2)
    outer(2, pc_c)

    def use3(i, h, v):
        x = 2 * i + h
        g = v * slope(pre[x]) * live[...]
        store(3, x, g)
        keep_t(i, h, g)

    conv(pc_c, w2f, use3)
    send(3)
    inner(3, pc_c)
    wgrad(pc_a, gw1_ref)
    arrive(3)
    outer(3, pc_c)

    def use4(i, h, v):
        x = 2 * i + h
        g = (fld[2, x].reshape(plane, ch).astype(F32) + v) * live[...]
        gin_ref[x] = g.astype(BF16).reshape(edge, rows, ch)

    conv(pc_c, w1f, use4)
    for f in range(4):
        drain(f)


def selection(nb, edge, slots):
    zero = jnp.arange(slots, dtype=jnp.int32)[:, None]
    full = jnp.concatenate([nb[:, :13], zero, nb[:, 13:]], axis=1).reshape(slots, 9, 3)
    full = jnp.transpose(full, (1, 2, 0))
    z = jnp.arange(edge)
    src = z[None, :] + jnp.arange(3)[:, None] - 1
    dz = jnp.where(src < 0, 0, jnp.where(src >= edge, 2, 1))
    pick = (dz[:, :, None] == jnp.arange(3)).astype(jnp.int32)
    target = jnp.sum(pick[None, :, None, :, :] * jnp.transpose(full, (0, 2, 1))[:, None, :, None, :], axis=-1)
    hit = (target[..., None, None] == jnp.arange(slots)[:, None]) & (
        (src % edge)[None, :, None, :, None, None] == z[None, :]
    )
    return hit.astype(BF16).reshape(9, 3 * slots * edge, slots * edge)


def flipped_weight(weight):
    return jnp.transpose(weight[::-1], (0, 2, 1))


def shards(nx, ny, nd, features, cotangent, first_weight, second_weight, neighbours, counts):
    _, edge, _, slots, _, ch = features.shape
    rows = slots * edge
    plane = edge * rows
    flat = (edge, edge, rows, ch)
    scale = float(nx * ny * nd * slots * edge**3) ** -0.5
    sel = selection(neighbours[0, 0, 0], edge, slots)
    ok = (jnp.arange(slots, dtype=jnp.int32) < counts[0, 0, 0]).astype(F32)
    live = jnp.broadcast_to(ok[None, :, None, None], (edge, slots, edge, ch)).reshape(plane, ch)
    wshape = (3, 9 * ch, ch)
    vmem = pl.BlockSpec(memory_space=pltpu.VMEM)
    gshape = jax.ShapeDtypeStruct((3, 3, ch, 3 * ch), F32)
    fshape = jax.ShapeDtypeStruct(flat, BF16)
    out, gin, g1, g2 = pl.pallas_call(
        functools.partial(kernel, nx, ny),
        out_shape=[fshape, fshape, gshape, gshape],
        in_specs=[vmem] * 8,
        out_specs=[vmem] * 4,
        scratch_shapes=[
            pltpu.VMEM((4,) + flat, BF16),
            pltpu.VMEM((4, 2, edge, rows, ch), BF16),
            pltpu.VMEM((4, 2, edge, rows, ch), BF16),
            pltpu.VMEM((4, 4, rows, ch), BF16),
            pltpu.VMEM((edge + 2, edge, rows, 9 * ch), BF16),
            pltpu.VMEM((edge + 2, edge, rows, 9 * ch), BF16),
            pltpu.VMEM((edge + 2, edge, rows, 9 * ch), BF16),
            pltpu.VMEM((edge, plane, ch), F32),
            pltpu.VMEM((2 * ch, edge // 2 * plane), BF16),
            pltpu.SemaphoreType.DMA((4, len(DIRS))),
            pltpu.SemaphoreType.DMA((4, len(DIRS))),
        ],
        compiler_params=pltpu.CompilerParams(
            collective_id=0, has_side_effects=True, vmem_limit_bytes=60 * 1024 * 1024
        ),
    )(
        features.reshape(flat),
        cotangent.reshape(flat),
        first_weight.reshape(wshape),
        second_weight.reshape(wshape),
        flipped_weight(first_weight).reshape(wshape),
        flipped_weight(second_weight).reshape(wshape),
        sel,
        live,
    )
    g1, g2 = lax.psum((g1, g2), ("sx", "sy", "dp"))

    def finish(g):
        g = g.reshape(9, ch, 3, ch)
        return jnp.transpose(g, (0, 2, 3, 1)).reshape(27, ch, ch) * scale

    return out.reshape(features.shape), gin.reshape(features.shape), finish(g1), finish(g2)


def solution(mesh):
    field = P("dp", "sx", "sy", None, None, None)
    return jax.shard_map(
        functools.partial(shards, mesh.shape["sx"], mesh.shape["sy"], mesh.shape["dp"]),
        mesh=mesh,
        in_specs=(field, field, P(), P(), P("dp", "sx", "sy", None, None), P("dp", "sx", "sy")),
        out_specs=(field, field, P(), P()),
        check_vma=False,
    )
```

```python
import functools

import jax
import jax.numpy as jnp
from jax import lax
from jax.experimental import pallas as pl
from jax.experimental.pallas import tpu as pltpu
from jax.sharding import PartitionSpec as P

DIRS = [(dx, dy) for dx in (-1, 0, 1) for dy in (-1, 0, 1) if (dx, dy) != (0, 0)]
F32 = jnp.float32
BF16 = jnp.bfloat16
UNIT = 16


def slope(v):
    s = jax.nn.sigmoid(v)
    return s * (1.0 + v * (1.0 - s))


def kernel(
    nx,
    ny,
    nd,
    feat,
    cot,
    w1,
    w2,
    w1f,
    w2f,
    sel,
    live,
    out_ref,
    gin_ref,
    gw1_ref,
    gw2_ref,
    fld,
    rx,
    ry,
    rc,
    pc_a,
    pc_b,
    pc_c,
    pre,
    gt,
    send_sem,
    recv_sem,
    gb,
    dx_buf,
    hs,
    rb,
    fin,
    pair_send,
    pair_recv,
    rs_send,
    rs_recv,
    ag_send,
    ag_recv,
    fw_send,
    fw_recv,
):
    edge = feat.shape[0]
    rows = feat.shape[2]
    ch = feat.shape[3]
    pairs = edge // 2
    plane = edge * rows
    ix = lax.axis_index("sx")
    iy = lax.axis_index("sy")

    def there(dx, dy):
        ok = None
        for d, i, n in ((dx, ix, nx), (dy, iy, ny)):
            if d == 0:
                continue
            c = (i < n - 1) if d > 0 else (i > 0)
            ok = c if ok is None else jnp.logical_and(ok, c)
        return ok

    def peer(dx, dy):
        px = jnp.minimum(jnp.maximum(ix + dx, 0), nx - 1)
        py = jnp.minimum(jnp.maximum(iy + dy, 0), ny - 1)
        return {"sx": px, "sy": py}

    def halo_ref(f, dx, dy):
        if dy == 0:
            return rx.at[f, (dx + 1) // 2]
        if dx == 0:
            return ry.at[f, (dy + 1) // 2]
        return rc.at[f, (dx + 1) // 2 * 2 + (dy + 1) // 2]

    def desc(f, k):
        dx, dy = DIRS[k]
        far_x = edge - 1 if dx > 0 else 0
        far_y = edge - 1 if dy > 0 else 0
        if dy == 0:
            src = fld.at[f, far_x]
        elif dx == 0:
            src = fld.at[f, :, far_y]
        else:
            src = fld.at[f, far_x, far_y]
        return pltpu.make_async_remote_copy(
            src_ref=src,
            dst_ref=halo_ref(f, -dx, -dy),
            send_sem=send_sem.at[f, k],
            recv_sem=recv_sem.at[f, k],
            device_id=peer(dx, dy),
            device_id_type=pl.DeviceIdType.MESH,
        )

    def send(f):
        for k, (dx, dy) in enumerate(DIRS):
            @pl.when(there(dx, dy))
            def _(k=k):
                desc(f, k).start()

    def arrive(f):
        for k, (dx, dy) in enumerate(DIRS):
            @pl.when(there(-dx, -dy))
            def _(k=k):
                desc(f, k).wait_recv()

    def drain(f):
        for k, (dx, dy) in enumerate(DIRS):
            @pl.when(there(dx, dy))
            def _(k=k):
                desc(f, k).wait_send()

    def put(pc, x, yp, tile):
        t = tile.astype(BF16)
        for b in range(3):
            y = yp - b
            if 0 <= y < edge:
                for c in range(3):
                    lo = (b * 3 + c) * ch
                    pc[x, y, :, lo : lo + ch] = t[c * rows : (c + 1) * rows]

    def line(pc, x, s, tiles):
        cat = jnp.concatenate(tiles, axis=1)
        got = jnp.dot(s, cat, preferred_element_type=F32)
        for y in range(edge):
            put(pc, x, y + 1, got[:, y * ch : (y + 1) * ch])

    def inner(f, pc):
        def body(x, carry):
            line(pc, x + 1, sel[4], [fld[f, x, y] for y in range(edge)])
            return carry

        lax.fori_loop(0, edge, body, 0)

    def outer(f, pc):
        for h in range(2):
            x = 0 if h == 0 else edge + 1
            line(pc, x, sel[6 * h + 1], [rx[f, h, y] for y in range(edge)])
            for g in range(2):
                yp = 0 if g == 0 else edge + 1
                put(pc, x, yp, jnp.dot(sel[6 * h + 2 * g], rc[f, h * 2 + g], preferred_element_type=F32))
            cat = jnp.concatenate([ry[f, h, x] for x in range(edge)], axis=1)
            got = jnp.dot(sel[3 + 2 * h], cat, preferred_element_type=F32)
            for x in range(edge):
                put(pc, x + 1, 0 if h == 0 else edge + 1, got[:, x * ch : (x + 1) * ch])

    def conv(pc, w, use):
        def body(i, carry):
            left = None
            right = None
            for p in range(4):
                lhs = pc[2 * i + p].reshape(plane, 9 * ch)
                wl = w[p] if p < 3 else None
                wr = w[p - 1] if p > 0 else None
                if wr is None:
                    left = jnp.dot(lhs, wl, preferred_element_type=F32)
                elif wl is None:
                    right = right + jnp.dot(lhs, wr, preferred_element_type=F32)
                else:
                    both = jnp.dot(lhs, jnp.concatenate([wl, wr], axis=1), preferred_element_type=F32)
                    left = left + both[:, :ch]
                    right = both[:, ch:] if right is None else right + both[:, ch:]
            use(i, 0, left)
            use(i, 1, right)
            return carry

        lax.fori_loop(0, pairs, body, 0)

    def keep_t(i, h, v):
        gt[h * ch : (h + 1) * ch, pl.ds(pl.multiple_of(i * plane, plane), plane)] = v.T.astype(BF16)

    def tap_out(g, a, b, v):
        per = ch // UNIT
        for c in range(3):
            t = v[:, c * ch : (c + 1) * ch].T.astype(BF16).reshape(per, UNIT, ch)
            gb[g, pl.ds(((a * 3 + b) * 3 + c) * per, per)] = t

    def wgrad(pc, g):
        def body(b, carry):
            lanes = pl.ds(pl.multiple_of(b * (3 * ch), 3 * ch), 3 * ch)
            part = None
            for p in range(4):
                acc = None
                for i in range(pairs):
                    rhs = pc[2 * i + p, :, :, lanes].reshape(plane, 3 * ch)
                    lhs = gt[:, i * plane : (i + 1) * plane]
                    if p == 0:
                        lhs = lhs[:ch]
                    elif p == 3:
                        lhs = lhs[ch:]
                    t = jnp.dot(lhs, rhs, preferred_element_type=F32)
                    acc = t if acc is None else acc + t
                if p == 3:
                    tap_out(g, 2, b, part + acc)
                elif p > 0:
                    tap_out(g, p - 1, b, part + acc[ch:])
                if p < 3:
                    part = acc[:ch]
            return carry

        lax.fori_loop(0, 3, body, 0)

    n = nx * ny
    units = gb.shape[1]
    half = units // nd
    q = half // n
    core = lax.axis_index("dp")
    me = ix * ny + iy
    mesh_id = pl.DeviceIdType.MESH

    def group(p):
        return {"sx": p // ny, "sy": lax.rem(p, ny)}

    def pair_desc(g):
        return pltpu.make_async_remote_copy(
            src_ref=gb.at[g, pl.ds((1 - core) * half, half)],
            dst_ref=dx_buf.at[g],
            send_sem=pair_send.at[g],
            recv_sem=pair_recv.at[g],
            device_id={"dp": 1 - core},
            device_id_type=mesh_id,
        )

    def rs_desc(g, o):
        p = lax.rem(me + o, n)
        return pltpu.make_async_remote_copy(
            src_ref=hs.at[g, pl.ds(p * q, q)],
            dst_ref=rb.at[g, o],
            send_sem=rs_send.at[g, o],
            recv_sem=rs_recv.at[g, o],
            device_id=group(p),
            device_id_type=mesh_id,
        )

    def ag_desc(g, o, owner):
        here = pl.ds(core * half + owner * q, q)
        return pltpu.make_async_remote_copy(
            src_ref=fin.at[g, here],
            dst_ref=fin.at[g, here],
            send_sem=ag_send.at[g, o],
            recv_sem=ag_recv.at[g, o],
            device_id=group(lax.rem(me + o, n)),
            device_id_type=mesh_id,
        )

    def fw_desc(g, o, side):
        here = pl.ds(side * half + lax.rem(me + n - o, n) * q, q)
        return pltpu.make_async_remote_copy(
            src_ref=fin.at[g, here],
            dst_ref=fin.at[g, here],
            send_sem=fw_send.at[g, o],
            recv_sem=fw_recv.at[g, o],
            device_id={"dp": 1 - core},
            device_id_type=mesh_id,
        )

    def each(lo, hi, fn):
        def body(o, carry):
            fn(o)
            return carry

        lax.fori_loop(lo, hi, body, 0)

    def scatter(g):
        pair_desc(g).wait_recv()

        def one(o):
            p = lax.rem(me + o, n)
            mine = gb[g, pl.ds(core * half + p * q, q)].astype(F32)
            hs[g, pl.ds(p * q, q)] = (mine + dx_buf[g, pl.ds(p * q, q)].astype(F32)).astype(BF16)

        each(0, n, one)
        each(1, n, lambda o: rs_desc(g, o).start())

    def gather(g):
        each(1, n, lambda o: rs_desc(g, o).wait_recv())

        def add(o, acc):
            return acc + rb[g, o].astype(F32)

        total = lax.fori_loop(1, n, add, hs[g, pl.ds(me * q, q)].astype(F32))
        fin[g, pl.ds(core * half + me * q, q)] = total.astype(BF16)
        each(1, n, lambda o: ag_desc(g, o, me).start())
        fw_desc(g, 0, core).start()

    def forward(g):
        def one(o):
            ag_desc(g, o, lax.rem(me + n - o, n)).wait_recv()
            fw_desc(g, o, core).start()

        each(1, n, one)

    def finish(g, ref):
        each(0, n, lambda o: fw_desc(g, o, 1 - core).wait_recv())
        ref[...] = fin[g]

    def drain_sums(g):
        pair_desc(g).wait_send()

        def one(o):
            rs_desc(g, o).wait_send()
            ag_desc(g, o, me).wait_send()

        each(1, n, one)
        each(0, n, lambda o: fw_desc(g, o, core).wait_send())

    for dx, dy in DIRS:
        @pl.when(jnp.logical_not(there(dx, dy)))
        def _(dx=dx, dy=dy):
            for f in range(4):
                r = halo_ref(f, dx, dy)
                r[...] = jnp.zeros(r.shape, BF16)

    barrier = pltpu.get_barrier_semaphore()
    each(
        1,
        n,
        lambda o: pl.semaphore_signal(
            barrier, inc=1, device_id=group(lax.rem(me + o, n)), device_id_type=mesh_id
        ),
    )
    pl.semaphore_signal(barrier, inc=1, device_id={"dp": 1 - core}, device_id_type=mesh_id)

    spare = units - 27 * (ch // UNIT)
    if spare:
        for g in range(2):
            gb[g, units - spare :] = jnp.zeros((spare, UNIT, ch), BF16)

    def mask_in(x, carry):
        v = feat[x].astype(F32).reshape(plane, ch) * live[...]
        fld[0, x] = v.astype(BF16).reshape(edge, rows, ch)
        return carry

    lax.fori_loop(0, edge, mask_in, 0)

    pl.semaphore_wait(barrier, n)

    def store(f, x, v):
        fld[f, x] = v.astype(BF16).reshape(edge, rows, ch)

    send(0)
    inner(0, pc_a)
    arrive(0)
    outer(0, pc_a)

    def use1(i, h, v):
        x = 2 * i + h
        pre[x] = v
        store(1, x, v * jax.nn.sigmoid(v) * live[...])

    conv(pc_a, w1, use1)
    send(1)
    inner(1, pc_b)
    arrive(1)
    outer(1, pc_b)

    def use2(i, h, v):
        x = 2 * i + h
        v = v + fld[0, x].reshape(plane, ch).astype(F32)
        s = jax.nn.sigmoid(v)
        out_ref[x] = (v * s * live[...]).astype(BF16).reshape(edge, rows, ch)
        g = cot[x].reshape(plane, ch).astype(F32) * (s * (1.0 + v * (1.0 - s))) * live[...]
        store(2, x, g)
        keep_t(i, h, g)

    conv(pc_b, w2, use2)
    send(2)
    inner(2, pc_c)
    wgrad(pc_b, 0)
    pair_desc(0).start()
    arrive(2)
    outer(2, pc_c)
    scatter(0)

    def use3(i, h, v):
        x = 2 * i + h
        g = v * slope(pre[x]) * live[...]
        store(3, x, g)
        keep_t(i, h, g)

    conv(pc_c, w2f, use3)
    send(3)
    inner(3, pc_c)
    wgrad(pc_a, 1)
    pair_desc(1).start()
    gather(0)
    scatter(1)
    arrive(3)
    outer(3, pc_c)

    def use4(i, h, v):
        x = 2 * i + h
        g = (fld[2, x].reshape(plane, ch).astype(F32) + v) * live[...]
        gin_ref[x] = g.astype(BF16).reshape(edge, rows, ch)

    conv(pc_c, w1f, use4)
    gather(1)
    forward(0)
    forward(1)
    finish(0, gw2_ref)
    finish(1, gw1_ref)
    for f in range(4):
        drain(f)
    drain_sums(0)
    drain_sums(1)


def selection(nb, edge, slots):
    zero = jnp.arange(slots, dtype=jnp.int32)[:, None]
    full = jnp.concatenate([nb[:, :13], zero, nb[:, 13:]], axis=1).reshape(slots, 9, 3)
    full = jnp.transpose(full, (1, 2, 0))
    z = jnp.arange(edge)
    src = z[None, :] + jnp.arange(3)[:, None] - 1
    dz = jnp.where(src < 0, 0, jnp.where(src >= edge, 2, 1))
    pick = (dz[:, :, None] == jnp.arange(3)).astype(jnp.int32)
    target = jnp.sum(pick[None, :, None, :, :] * jnp.transpose(full, (0, 2, 1))[:, None, :, None, :], axis=-1)
    hit = (target[..., None, None] == jnp.arange(slots)[:, None]) & (
        (src % edge)[None, :, None, :, None, None] == z[None, :]
    )
    return hit.astype(BF16).reshape(9, 3 * slots * edge, slots * edge)


def flipped_weight(weight):
    return jnp.transpose(weight[::-1], (0, 2, 1))


def shards(nx, ny, nd, features, cotangent, first_weight, second_weight, neighbours, counts):
    _, edge, _, slots, _, ch = features.shape
    rows = slots * edge
    plane = edge * rows
    flat = (edge, edge, rows, ch)
    scale = float(nx * ny * nd * slots * edge**3) ** -0.5
    sel = selection(neighbours[0, 0, 0], edge, slots)
    ok = (jnp.arange(slots, dtype=jnp.int32) < counts[0, 0, 0]).astype(F32)
    live = jnp.broadcast_to(ok[None, :, None, None], (edge, slots, edge, ch)).reshape(plane, ch)
    wshape = (3, 9 * ch, ch)
    vmem = pl.BlockSpec(memory_space=pltpu.VMEM)
    n = nx * ny
    q = -(-27 * ch // (UNIT * n * nd))
    units = q * n * nd
    gshape = jax.ShapeDtypeStruct((units, UNIT, ch), BF16)
    fshape = jax.ShapeDtypeStruct(flat, BF16)
    out, gin, g1, g2 = pl.pallas_call(
        functools.partial(kernel, nx, ny, nd),
        out_shape=[fshape, fshape, gshape, gshape],
        in_specs=[vmem] * 8,
        out_specs=[vmem] * 4,
        scratch_shapes=[
            pltpu.VMEM((4,) + flat, BF16),
            pltpu.VMEM((4, 2, edge, rows, ch), BF16),
            pltpu.VMEM((4, 2, edge, rows, ch), BF16),
            pltpu.VMEM((4, 4, rows, ch), BF16),
            pltpu.VMEM((edge + 2, edge, rows, 9 * ch), BF16),
            pltpu.VMEM((edge + 2, edge, rows, 9 * ch), BF16),
            pltpu.VMEM((edge + 2, edge, rows, 9 * ch), BF16),
            pltpu.VMEM((edge, plane, ch), F32),
            pltpu.VMEM((2 * ch, edge // 2 * plane), BF16),
            pltpu.SemaphoreType.DMA((4, len(DIRS))),
            pltpu.SemaphoreType.DMA((4, len(DIRS))),
            pltpu.VMEM((2, units, UNIT, ch), BF16),
            pltpu.VMEM((2, units // nd, UNIT, ch), BF16),
            pltpu.VMEM((2, units // nd, UNIT, ch), BF16),
            pltpu.VMEM((2, n, q, UNIT, ch), BF16),
            pltpu.VMEM((2, units, UNIT, ch), BF16),
        ]
        + [pltpu.SemaphoreType.DMA((2,))] * 2
        + [pltpu.SemaphoreType.DMA((2, n))] * 6,
        compiler_params=pltpu.CompilerParams(
            collective_id=0, has_side_effects=True, vmem_limit_bytes=60 * 1024 * 1024
        ),
    )(
        features.reshape(flat),
        cotangent.reshape(flat),
        first_weight.reshape(wshape),
        second_weight.reshape(wshape),
        flipped_weight(first_weight).reshape(wshape),
        flipped_weight(second_weight).reshape(wshape),
        sel,
        live,
    )
    def finish(g):
        g = g.reshape(-1, ch)[: 27 * ch]
        return g.reshape(27, ch, ch).astype(F32) * scale

    return out.reshape(features.shape), gin.reshape(features.shape), finish(g1), finish(g2)


def solution(mesh):
    field = P("dp", "sx", "sy", None, None, None)
    return jax.shard_map(
        functools.partial(shards, mesh.shape["sx"], mesh.shape["sy"], mesh.shape["dp"]),
        mesh=mesh,
        in_specs=(field, field, P(), P(), P("dp", "sx", "sy", None, None), P("dp", "sx", "sy")),
        out_specs=(field, field, P(), P()),
        check_vma=False,
    )
```

```python
import functools

import jax
import jax.numpy as jnp
from jax import lax
from jax.experimental import pallas as pl
from jax.experimental.pallas import tpu as pltpu
from jax.sharding import PartitionSpec as P

DIRS = [(dx, dy) for dx in (-1, 0, 1) for dy in (-1, 0, 1) if (dx, dy) != (0, 0)]
F32 = jnp.float32
BF16 = jnp.bfloat16
UNIT = 16


def slope(v):
    s = jax.nn.sigmoid(v)
    return s * (1.0 + v * (1.0 - s))


def kernel(
    nx,
    ny,
    nd,
    feat,
    cot,
    w1,
    w2,
    nb,
    count,
    out_ref,
    gin_ref,
    gw1_ref,
    gw2_ref,
    fld,
    rx,
    ry,
    rc,
    pc_a,
    pc_b,
    pc_c,
    pre,
    gt,
    send_sem,
    recv_sem,
    w1f,
    w2f,
    sel,
    live,
    gb,
    dx_buf,
    hs,
    rb,
    fin,
    pair_send,
    pair_recv,
    rs_send,
    rs_recv,
    ag_send,
    ag_recv,
    fw_send,
    fw_recv,
):
    edge = feat.shape[0]
    rows = feat.shape[2]
    ch = feat.shape[3]
    pairs = edge // 2
    plane = edge * rows
    ix = lax.axis_index("sx")
    iy = lax.axis_index("sy")

    def there(dx, dy):
        ok = None
        for d, i, n in ((dx, ix, nx), (dy, iy, ny)):
            if d == 0:
                continue
            c = (i < n - 1) if d > 0 else (i > 0)
            ok = c if ok is None else jnp.logical_and(ok, c)
        return ok

    def peer(dx, dy):
        px = jnp.minimum(jnp.maximum(ix + dx, 0), nx - 1)
        py = jnp.minimum(jnp.maximum(iy + dy, 0), ny - 1)
        return {"sx": px, "sy": py}

    def halo_ref(f, dx, dy):
        if dy == 0:
            return rx.at[f, (dx + 1) // 2]
        if dx == 0:
            return ry.at[f, (dy + 1) // 2]
        return rc.at[f, (dx + 1) // 2 * 2 + (dy + 1) // 2]

    def desc(f, k):
        dx, dy = DIRS[k]
        far_x = edge - 1 if dx > 0 else 0
        far_y = edge - 1 if dy > 0 else 0
        if dy == 0:
            src = fld.at[f, far_x]
        elif dx == 0:
            src = fld.at[f, :, far_y]
        else:
            src = fld.at[f, far_x, far_y]
        return pltpu.make_async_remote_copy(
            src_ref=src,
            dst_ref=halo_ref(f, -dx, -dy),
            send_sem=send_sem.at[f, k],
            recv_sem=recv_sem.at[f, k],
            device_id=peer(dx, dy),
            device_id_type=pl.DeviceIdType.MESH,
        )

    def send(f):
        for k, (dx, dy) in enumerate(DIRS):
            @pl.when(there(dx, dy))
            def _(k=k):
                desc(f, k).start()

    def arrive(f):
        for k, (dx, dy) in enumerate(DIRS):
            @pl.when(there(-dx, -dy))
            def _(k=k):
                desc(f, k).wait_recv()

    def drain(f):
        for k, (dx, dy) in enumerate(DIRS):
            @pl.when(there(dx, dy))
            def _(k=k):
                desc(f, k).wait_send()

    def put(pc, x, yp, tile):
        t = tile.astype(BF16)
        for b in range(3):
            y = yp - b
            if 0 <= y < edge:
                for c in range(3):
                    lo = (b * 3 + c) * ch
                    pc[x, y, :, lo : lo + ch] = t[c * rows : (c + 1) * rows]

    def line(pc, x, s, tiles):
        cat = jnp.concatenate(tiles, axis=1)
        got = jnp.dot(s, cat, preferred_element_type=F32)
        for y in range(edge):
            put(pc, x, y + 1, got[:, y * ch : (y + 1) * ch])

    def inner(f, pc):
        def body(x, carry):
            line(pc, x + 1, sel[4], [fld[f, x, y] for y in range(edge)])
            return carry

        lax.fori_loop(0, edge, body, 0)

    def outer(f, pc):
        for h in range(2):
            x = 0 if h == 0 else edge + 1
            line(pc, x, sel[6 * h + 1], [rx[f, h, y] for y in range(edge)])
            for g in range(2):
                yp = 0 if g == 0 else edge + 1
                put(pc, x, yp, jnp.dot(sel[6 * h + 2 * g], rc[f, h * 2 + g], preferred_element_type=F32))
            cat = jnp.concatenate([ry[f, h, x] for x in range(edge)], axis=1)
            got = jnp.dot(sel[3 + 2 * h], cat, preferred_element_type=F32)
            for x in range(edge):
                put(pc, x + 1, 0 if h == 0 else edge + 1, got[:, x * ch : (x + 1) * ch])

    def conv(pc, w, use):
        def body(i, carry):
            left = None
            right = None
            for p in range(4):
                lhs = pc[2 * i + p].reshape(plane, 9 * ch)
                wl = w[9 * p : 9 * p + 9].reshape(9 * ch, ch) if p < 3 else None
                wr = w[9 * p - 9 : 9 * p].reshape(9 * ch, ch) if p > 0 else None
                if wr is None:
                    left = jnp.dot(lhs, wl, preferred_element_type=F32)
                elif wl is None:
                    right = right + jnp.dot(lhs, wr, preferred_element_type=F32)
                else:
                    both = jnp.dot(lhs, jnp.concatenate([wl, wr], axis=1), preferred_element_type=F32)
                    left = left + both[:, :ch]
                    right = both[:, ch:] if right is None else right + both[:, ch:]
            use(i, 0, left)
            use(i, 1, right)
            return carry

        lax.fori_loop(0, pairs, body, 0)

    def keep_t(i, h, v):
        gt[h * ch : (h + 1) * ch, pl.ds(pl.multiple_of(i * plane, plane), plane)] = v.T.astype(BF16)

    def tap_out(g, a, b, v):
        per = ch // UNIT
        for c in range(3):
            t = v[:, c * ch : (c + 1) * ch].T.astype(BF16).reshape(per, UNIT, ch)
            gb[g, pl.ds(((a * 3 + b) * 3 + c) * per, per)] = t

    def wgrad(pc, g):
        def body(b, carry):
            lanes = pl.ds(pl.multiple_of(b * (3 * ch), 3 * ch), 3 * ch)
            part = None
            for p in range(4):
                acc = None
                for i in range(pairs):
                    rhs = pc[2 * i + p, :, :, lanes].reshape(plane, 3 * ch)
                    lhs = gt[:, i * plane : (i + 1) * plane]
                    if p == 0:
                        lhs = lhs[:ch]
                    elif p == 3:
                        lhs = lhs[ch:]
                    t = jnp.dot(lhs, rhs, preferred_element_type=F32)
                    acc = t if acc is None else acc + t
                if p == 3:
                    tap_out(g, 2, b, part + acc)
                elif p > 0:
                    tap_out(g, p - 1, b, part + acc[ch:])
                if p < 3:
                    part = acc[:ch]
            return carry

        lax.fori_loop(0, 3, body, 0)

    n = nx * ny
    units = gb.shape[1]
    half = units // nd
    q = half // n
    core = lax.axis_index("dp")
    me = ix * ny + iy
    mesh_id = pl.DeviceIdType.MESH

    def group(p):
        return {"sx": p // ny, "sy": lax.rem(p, ny)}

    def pair_desc(g):
        return pltpu.make_async_remote_copy(
            src_ref=gb.at[g, pl.ds((1 - core) * half, half)],
            dst_ref=dx_buf.at[g],
            send_sem=pair_send.at[g],
            recv_sem=pair_recv.at[g],
            device_id={"dp": 1 - core},
            device_id_type=mesh_id,
        )

    def rs_desc(g, o):
        p = lax.rem(me + o, n)
        return pltpu.make_async_remote_copy(
            src_ref=hs.at[g, pl.ds(p * q, q)],
            dst_ref=rb.at[g, o],
            send_sem=rs_send.at[g, o],
            recv_sem=rs_recv.at[g, o],
            device_id=group(p),
            device_id_type=mesh_id,
        )

    def ag_desc(g, o, owner):
        here = pl.ds(core * half + owner * q, q)
        return pltpu.make_async_remote_copy(
            src_ref=fin.at[g, here],
            dst_ref=fin.at[g, here],
            send_sem=ag_send.at[g, o],
            recv_sem=ag_recv.at[g, o],
            device_id=group(lax.rem(me + o, n)),
            device_id_type=mesh_id,
        )

    def fw_desc(g, o, side):
        here = pl.ds(side * half + lax.rem(me + n - o, n) * q, q)
        return pltpu.make_async_remote_copy(
            src_ref=fin.at[g, here],
            dst_ref=fin.at[g, here],
            send_sem=fw_send.at[g, o],
            recv_sem=fw_recv.at[g, o],
            device_id={"dp": 1 - core},
            device_id_type=mesh_id,
        )

    def each(lo, hi, fn):
        def body(o, carry):
            fn(o)
            return carry

        lax.fori_loop(lo, hi, body, 0)

    def scatter(g):
        pair_desc(g).wait_recv()

        def one(o):
            p = lax.rem(me + o, n)
            mine = gb[g, pl.ds(core * half + p * q, q)].astype(F32)
            hs[g, pl.ds(p * q, q)] = (mine + dx_buf[g, pl.ds(p * q, q)].astype(F32)).astype(BF16)

        each(0, n, one)
        each(1, n, lambda o: rs_desc(g, o).start())

    def gather(g):
        each(1, n, lambda o: rs_desc(g, o).wait_recv())

        def add(o, acc):
            return acc + rb[g, o].astype(F32)

        total = lax.fori_loop(1, n, add, hs[g, pl.ds(me * q, q)].astype(F32))
        fin[g, pl.ds(core * half + me * q, q)] = total.astype(BF16)
        each(1, n, lambda o: ag_desc(g, o, me).start())
        fw_desc(g, 0, core).start()

    def forward(g):
        def one(o):
            ag_desc(g, o, lax.rem(me + n - o, n)).wait_recv()
            fw_desc(g, o, core).start()

        each(1, n, one)

    def finish(g, ref):
        each(0, n, lambda o: fw_desc(g, o, 1 - core).wait_recv())
        ref[...] = fin[g]

    def drain_sums(g):
        pair_desc(g).wait_send()

        def one(o):
            rs_desc(g, o).wait_send()
            ag_desc(g, o, me).wait_send()

        each(1, n, one)
        each(0, n, lambda o: fw_desc(g, o, core).wait_send())

    for dx, dy in DIRS:
        @pl.when(jnp.logical_not(there(dx, dy)))
        def _(dx=dx, dy=dy):
            for f in range(4):
                r = halo_ref(f, dx, dy)
                r[...] = jnp.zeros(r.shape, BF16)

    barrier = pltpu.get_barrier_semaphore()
    each(
        1,
        n,
        lambda o: pl.semaphore_signal(
            barrier, inc=1, device_id=group(lax.rem(me + o, n)), device_id_type=mesh_id
        ),
    )
    pl.semaphore_signal(barrier, inc=1, device_id={"dp": 1 - core}, device_id_type=mesh_id)

    spare = units - 27 * (ch // UNIT)
    if spare:
        for g in range(2):
            gb[g, units - spare :] = jnp.zeros((spare, UNIT, ch), BF16)

    slots = rows // edge
    row = lax.broadcasted_iota(jnp.int32, (plane, ch), 0)
    live[...] = jnp.where(lax.rem(lax.div(row, edge), slots) < count[0], 1.0, 0.0).astype(F32)

    r = lax.broadcasted_iota(jnp.int32, (3 * rows, rows), 0)
    col = lax.broadcasted_iota(jnp.int32, (3 * rows, rows), 1)
    src = lax.rem(r, edge) + lax.div(r, rows) - 1
    dz = jnp.where(src < 0, 0, jnp.where(src >= edge, 2, 1))
    key = dz * slots + lax.rem(lax.div(r, edge), slots)
    same_z = lax.rem(src + edge, edge) == lax.rem(col, edge)
    slot = lax.div(col, edge)
    for d in range(9):
        target = jnp.full((3 * rows, rows), -1, jnp.int32)
        for k in range(3):
            way = d * 3 + k
            for sl in range(slots):
                name = sl if way == 13 else nb[sl, way if way < 13 else way - 1]
                target = jnp.where(key == k * slots + sl, name, target)
        hit = jnp.logical_and(same_z, target == slot)
        sel[d] = jnp.where(hit, 1.0, 0.0).astype(F32).astype(BF16)

    def flip(w, to):
        def body(k, carry):
            to[k] = w[26 - k].astype(F32).T.astype(BF16)
            return carry

        lax.fori_loop(0, 27, body, 0)

    def mask_in(x, carry):
        v = feat[x].astype(F32).reshape(plane, ch) * live[...]
        fld[0, x] = v.astype(BF16).reshape(edge, rows, ch)
        return carry

    lax.fori_loop(0, edge, mask_in, 0)

    pl.semaphore_wait(barrier, n)

    def store(f, x, v):
        fld[f, x] = v.astype(BF16).reshape(edge, rows, ch)

    send(0)
    inner(0, pc_a)
    flip(w2, w2f)
    arrive(0)
    outer(0, pc_a)

    def use1(i, h, v):
        x = 2 * i + h
        pre[x] = v
        store(1, x, v * jax.nn.sigmoid(v) * live[...])

    conv(pc_a, w1, use1)
    send(1)
    inner(1, pc_b)
    flip(w1, w1f)
    arrive(1)
    outer(1, pc_b)

    def use2(i, h, v):
        x = 2 * i + h
        v = v + fld[0, x].reshape(plane, ch).astype(F32)
        s = jax.nn.sigmoid(v)
        out_ref[x] = (v * s * live[...]).astype(BF16).reshape(edge, rows, ch)
        g = cot[x].reshape(plane, ch).astype(F32) * (s * (1.0 + v * (1.0 - s))) * live[...]
        store(2, x, g)
        keep_t(i, h, g)

    conv(pc_b, w2, use2)
    send(2)
    inner(2, pc_c)
    wgrad(pc_b, 0)
    pair_desc(0).start()
    arrive(2)
    outer(2, pc_c)
    scatter(0)

    def use3(i, h, v):
        x = 2 * i + h
        g = v * slope(pre[x]) * live[...]
        store(3, x, g)
        keep_t(i, h, g)

    conv(pc_c, w2f, use3)
    send(3)
    gather(0)
    wgrad(pc_a, 1)
    pair_desc(1).start()
    inner(3, pc_c)
    scatter(1)
    arrive(3)
    outer(3, pc_c)
    forward(0)

    def use4(i, h, v):
        x = 2 * i + h
        g = (fld[2, x].reshape(plane, ch).astype(F32) + v) * live[...]
        gin_ref[x] = g.astype(BF16).reshape(edge, rows, ch)

    conv(pc_c, w1f, use4)
    gather(1)
    forward(1)
    finish(0, gw2_ref)
    finish(1, gw1_ref)
    for f in range(4):
        drain(f)
    drain_sums(0)
    drain_sums(1)


def shards(nx, ny, nd, features, cotangent, first_weight, second_weight, neighbours, counts):
    _, edge, _, slots, _, ch = features.shape
    rows = slots * edge
    plane = edge * rows
    flat = (edge, edge, rows, ch)
    scale = float(nx * ny * nd * slots * edge**3) ** -0.5
    vmem = pl.BlockSpec(memory_space=pltpu.VMEM)
    smem = pl.BlockSpec(memory_space=pltpu.SMEM)
    n = nx * ny
    q = -(-27 * ch // (UNIT * n * nd))
    units = q * n * nd
    gshape = jax.ShapeDtypeStruct((units, UNIT, ch), BF16)
    fshape = jax.ShapeDtypeStruct(flat, BF16)
    out, gin, g1, g2 = pl.pallas_call(
        functools.partial(kernel, nx, ny, nd),
        out_shape=[fshape, fshape, gshape, gshape],
        in_specs=[vmem] * 4 + [smem] * 2,
        out_specs=[vmem] * 4,
        scratch_shapes=[
            pltpu.VMEM((4,) + flat, BF16),
            pltpu.VMEM((4, 2, edge, rows, ch), BF16),
            pltpu.VMEM((4, 2, edge, rows, ch), BF16),
            pltpu.VMEM((4, 4, rows, ch), BF16),
            pltpu.VMEM((edge + 2, edge, rows, 9 * ch), BF16),
            pltpu.VMEM((edge + 2, edge, rows, 9 * ch), BF16),
            pltpu.VMEM((edge + 2, edge, rows, 9 * ch), BF16),
            pltpu.VMEM((edge, plane, ch), F32),
            pltpu.VMEM((2 * ch, edge // 2 * plane), BF16),
            pltpu.SemaphoreType.DMA((4, len(DIRS))),
            pltpu.SemaphoreType.DMA((4, len(DIRS))),
            pltpu.VMEM((27, ch, ch), BF16),
            pltpu.VMEM((27, ch, ch), BF16),
            pltpu.VMEM((9, 3 * rows, rows), BF16),
            pltpu.VMEM((plane, ch), F32),
            pltpu.VMEM((2, units, UNIT, ch), BF16),
            pltpu.VMEM((2, units // nd, UNIT, ch), BF16),
            pltpu.VMEM((2, units // nd, UNIT, ch), BF16),
            pltpu.VMEM((2, n, q, UNIT, ch), BF16),
            pltpu.VMEM((2, units, UNIT, ch), BF16),
        ]
        + [pltpu.SemaphoreType.DMA((2,))] * 2
        + [pltpu.SemaphoreType.DMA((2, n))] * 6,
        compiler_params=pltpu.CompilerParams(
            collective_id=0, has_side_effects=True, vmem_limit_bytes=60 * 1024 * 1024
        ),
    )(
        features.reshape(flat),
        cotangent.reshape(flat),
        first_weight,
        second_weight,
        neighbours[0, 0, 0],
        counts.reshape(1),
    )
    def finish(g):
        g = g.reshape(-1, ch)[: 27 * ch]
        return g.reshape(27, ch, ch).astype(F32) * scale

    return out.reshape(features.shape), gin.reshape(features.shape), finish(g1), finish(g2)


def solution(mesh):
    field = P("dp", "sx", "sy", None, None, None)
    return jax.shard_map(
        functools.partial(shards, mesh.shape["sx"], mesh.shape["sy"], mesh.shape["dp"]),
        mesh=mesh,
        in_specs=(field, field, P(), P(), P("dp", "sx", "sy", None, None), P("dp", "sx", "sy")),
        out_specs=(field, field, P(), P()),
        check_vma=False,
    )
```

```python
import functools

import jax
import jax.numpy as jnp
from jax import lax
from jax.experimental import pallas as pl
from jax.experimental.pallas import tpu as pltpu
from jax.sharding import PartitionSpec as P

DIRS = [(dx, dy) for dx in (-1, 0, 1) for dy in (-1, 0, 1) if (dx, dy) != (0, 0)]
F32 = jnp.float32
BF16 = jnp.bfloat16
UNIT = 16


def slope(v):
    s = jax.nn.sigmoid(v)
    return s * (1.0 + v * (1.0 - s))


def kernel(
    nx,
    ny,
    nd,
    feat,
    cot,
    w1,
    w2,
    nb,
    count,
    out_ref,
    gin_ref,
    gw1_ref,
    gw2_ref,
    fld,
    rx,
    ry,
    rc,
    pc_a,
    pc_b,
    pc_c,
    pre,
    gt,
    send_sem,
    recv_sem,
    w1f,
    w2f,
    sel,
    live,
    gb,
    dx_buf,
    hs,
    rb,
    fin,
    pair_send,
    pair_recv,
    rs_send,
    rs_recv,
    ag_send,
    ag_recv,
    fw_send,
    fw_recv,
):
    edge = feat.shape[0]
    rows = feat.shape[2]
    ch = feat.shape[3]
    pairs = edge // 2
    plane = edge * rows
    ix = lax.axis_index("sx")
    iy = lax.axis_index("sy")

    def there(dx, dy):
        ok = None
        for d, i, n in ((dx, ix, nx), (dy, iy, ny)):
            if d == 0:
                continue
            c = (i < n - 1) if d > 0 else (i > 0)
            ok = c if ok is None else jnp.logical_and(ok, c)
        return ok

    def peer(dx, dy):
        px = jnp.minimum(jnp.maximum(ix + dx, 0), nx - 1)
        py = jnp.minimum(jnp.maximum(iy + dy, 0), ny - 1)
        return {"sx": px, "sy": py}

    def halo_ref(f, dx, dy):
        if dy == 0:
            return rx.at[f, (dx + 1) // 2]
        if dx == 0:
            return ry.at[f, (dy + 1) // 2]
        return rc.at[f, (dx + 1) // 2 * 2 + (dy + 1) // 2]

    def desc(f, k):
        dx, dy = DIRS[k]
        far_x = edge - 1 if dx > 0 else 0
        far_y = edge - 1 if dy > 0 else 0
        if dy == 0:
            src = fld.at[f, far_x]
        elif dx == 0:
            src = fld.at[f, :, far_y]
        else:
            src = fld.at[f, far_x, far_y]
        return pltpu.make_async_remote_copy(
            src_ref=src,
            dst_ref=halo_ref(f, -dx, -dy),
            send_sem=send_sem.at[f, k],
            recv_sem=recv_sem.at[f, k],
            device_id=peer(dx, dy),
            device_id_type=pl.DeviceIdType.MESH,
        )

    def send(f):
        for k, (dx, dy) in enumerate(DIRS):
            @pl.when(there(dx, dy))
            def _(k=k):
                desc(f, k).start()

    def arrive(f):
        for k, (dx, dy) in enumerate(DIRS):
            @pl.when(there(-dx, -dy))
            def _(k=k):
                desc(f, k).wait_recv()

    def drain(f):
        for k, (dx, dy) in enumerate(DIRS):
            @pl.when(there(dx, dy))
            def _(k=k):
                desc(f, k).wait_send()

    def put(pc, x, yp, tile):
        t = tile.astype(BF16)
        for b in range(3):
            y = yp - b
            if 0 <= y < edge:
                for c in range(3):
                    lo = (b * 3 + c) * ch
                    pc[x, y, :, lo : lo + ch] = t[c * rows : (c + 1) * rows]

    def line(pc, x, s, tiles):
        cat = jnp.concatenate(tiles, axis=1)
        got = jnp.dot(s, cat, preferred_element_type=F32)
        for y in range(edge):
            put(pc, x, y + 1, got[:, y * ch : (y + 1) * ch])

    def inner(f, pc):
        def body(x, carry):
            line(pc, x + 1, sel[4], [fld[f, x, y] for y in range(edge)])
            return carry

        lax.fori_loop(0, edge, body, 0)

    def outer(f, pc):
        for h in range(2):
            x = 0 if h == 0 else edge + 1
            line(pc, x, sel[6 * h + 1], [rx[f, h, y] for y in range(edge)])
            for g in range(2):
                yp = 0 if g == 0 else edge + 1
                put(pc, x, yp, jnp.dot(sel[6 * h + 2 * g], rc[f, h * 2 + g], preferred_element_type=F32))
            cat = jnp.concatenate([ry[f, h, x] for x in range(edge)], axis=1)
            got = jnp.dot(sel[3 + 2 * h], cat, preferred_element_type=F32)
            for x in range(edge):
                put(pc, x + 1, 0 if h == 0 else edge + 1, got[:, x * ch : (x + 1) * ch])

    def conv(pc, w, use):
        def body(i, carry):
            left = None
            right = None
            for p in range(4):
                lhs = pc[2 * i + p].reshape(plane, 9 * ch)
                wl = w[9 * p : 9 * p + 9].reshape(9 * ch, ch) if p < 3 else None
                wr = w[9 * p - 9 : 9 * p].reshape(9 * ch, ch) if p > 0 else None
                if wr is None:
                    left = jnp.dot(lhs, wl, preferred_element_type=F32)
                elif wl is None:
                    right = right + jnp.dot(lhs, wr, preferred_element_type=F32)
                else:
                    both = jnp.dot(lhs, jnp.concatenate([wl, wr], axis=1), preferred_element_type=F32)
                    left = left + both[:, :ch]
                    right = both[:, ch:] if right is None else right + both[:, ch:]
            use(i, 0, left)
            use(i, 1, right)
            return carry

        lax.fori_loop(0, pairs, body, 0)

    def keep_t(i, h, v):
        gt[h * ch : (h + 1) * ch, pl.ds(pl.multiple_of(i * plane, plane), plane)] = v.T.astype(BF16)

    def tap_out(g, a, b, v):
        per = ch // UNIT
        for c in range(3):
            t = v[:, c * ch : (c + 1) * ch].T.astype(BF16).reshape(per, UNIT, ch)
            gb[g, pl.ds(((a * 3 + b) * 3 + c) * per, per)] = t

    def wgrad(pc, g, lo, hi):
        def body(b, carry):
            lanes = pl.ds(pl.multiple_of(b * (3 * ch), 3 * ch), 3 * ch)
            part = None
            for p in range(4):
                acc = None
                for i in range(pairs):
                    rhs = pc[2 * i + p, :, :, lanes].reshape(plane, 3 * ch)
                    lhs = gt[:, i * plane : (i + 1) * plane]
                    if p == 0:
                        lhs = lhs[:ch]
                    elif p == 3:
                        lhs = lhs[ch:]
                    t = jnp.dot(lhs, rhs, preferred_element_type=F32)
                    acc = t if acc is None else acc + t
                if p == 3:
                    tap_out(g, 2, b, part + acc)
                elif p > 0:
                    tap_out(g, p - 1, b, part + acc[ch:])
                if p < 3:
                    part = acc[:ch]
            return carry

        lax.fori_loop(lo, hi, body, 0)

    n = nx * ny
    units = gb.shape[1]
    half = units // nd
    q = half // n
    core = lax.axis_index("dp")
    me = ix * ny + iy
    mesh_id = pl.DeviceIdType.MESH

    def group(p):
        return {"sx": p // ny, "sy": lax.rem(p, ny)}

    def pair_desc(g):
        return pltpu.make_async_remote_copy(
            src_ref=gb.at[g, pl.ds((1 - core) * half, half)],
            dst_ref=dx_buf.at[g],
            send_sem=pair_send.at[g],
            recv_sem=pair_recv.at[g],
            device_id={"dp": 1 - core},
            device_id_type=mesh_id,
        )

    def rs_desc(g, o):
        p = lax.rem(me + o, n)
        return pltpu.make_async_remote_copy(
            src_ref=hs.at[g, pl.ds(p * q, q)],
            dst_ref=rb.at[g, o],
            send_sem=rs_send.at[g, o],
            recv_sem=rs_recv.at[g, o],
            device_id=group(p),
            device_id_type=mesh_id,
        )

    def ag_desc(g, o, owner):
        here = pl.ds(core * half + owner * q, q)
        return pltpu.make_async_remote_copy(
            src_ref=fin.at[g, here],
            dst_ref=fin.at[g, here],
            send_sem=ag_send.at[g, o],
            recv_sem=ag_recv.at[g, o],
            device_id=group(lax.rem(me + o, n)),
            device_id_type=mesh_id,
        )

    def fw_desc(g, o, side):
        here = pl.ds(side * half + lax.rem(me + n - o, n) * q, q)
        return pltpu.make_async_remote_copy(
            src_ref=fin.at[g, here],
            dst_ref=fin.at[g, here],
            send_sem=fw_send.at[g, o],
            recv_sem=fw_recv.at[g, o],
            device_id={"dp": 1 - core},
            device_id_type=mesh_id,
        )

    def each(lo, hi, fn):
        def body(o, carry):
            fn(o)
            return carry

        lax.fori_loop(lo, hi, body, 0)

    def scatter(g):
        pair_desc(g).wait_recv()

        def one(o):
            p = lax.rem(me + o, n)
            mine = gb[g, pl.ds(core * half + p * q, q)].astype(F32)
            hs[g, pl.ds(p * q, q)] = (mine + dx_buf[g, pl.ds(p * q, q)].astype(F32)).astype(BF16)

        def go(o):
            one(o)
            rs_desc(g, o).start()

        each(1, n, go)
        one(0)

    def gather(g):
        each(1, n, lambda o: rs_desc(g, o).wait_recv())

        def add(o, acc):
            return acc + rb[g, o].astype(F32)

        total = lax.fori_loop(1, n, add, hs[g, pl.ds(me * q, q)].astype(F32))
        fin[g, pl.ds(core * half + me * q, q)] = total.astype(BF16)
        each(1, n, lambda o: ag_desc(g, o, me).start())
        fw_desc(g, 0, core).start()

    def forward(g):
        def one(o):
            ag_desc(g, o, lax.rem(me + n - o, n)).wait_recv()
            fw_desc(g, o, core).start()

        each(1, n, one)

    def finish(g, ref):
        each(0, n, lambda o: fw_desc(g, o, 1 - core).wait_recv())
        ref[...] = fin[g]

    def drain_sums(g):
        pair_desc(g).wait_send()

        def one(o):
            rs_desc(g, o).wait_send()
            ag_desc(g, o, me).wait_send()

        each(1, n, one)
        each(0, n, lambda o: fw_desc(g, o, core).wait_send())

    for dx, dy in DIRS:
        @pl.when(jnp.logical_not(there(dx, dy)))
        def _(dx=dx, dy=dy):
            for f in range(4):
                r = halo_ref(f, dx, dy)
                r[...] = jnp.zeros(r.shape, BF16)

    barrier = pltpu.get_barrier_semaphore()
    each(
        1,
        n,
        lambda o: pl.semaphore_signal(
            barrier, inc=1, device_id=group(lax.rem(me + o, n)), device_id_type=mesh_id
        ),
    )
    pl.semaphore_signal(barrier, inc=1, device_id={"dp": 1 - core}, device_id_type=mesh_id)

    spare = units - 27 * (ch // UNIT)
    if spare:
        for g in range(2):
            gb[g, units - spare :] = jnp.zeros((spare, UNIT, ch), BF16)

    slots = rows // edge
    row = lax.broadcasted_iota(jnp.int32, (plane, ch), 0)
    live[...] = jnp.where(lax.rem(lax.div(row, edge), slots) < count[0], 1.0, 0.0).astype(F32)

    r = lax.broadcasted_iota(jnp.int32, (3 * rows, rows), 0)
    col = lax.broadcasted_iota(jnp.int32, (3 * rows, rows), 1)
    src = lax.rem(r, edge) + lax.div(r, rows) - 1
    dz = jnp.where(src < 0, 0, jnp.where(src >= edge, 2, 1))
    key = dz * slots + lax.rem(lax.div(r, edge), slots)
    same_z = lax.rem(src + edge, edge) == lax.rem(col, edge)
    slot = lax.div(col, edge)
    for d in range(9):
        target = jnp.full((3 * rows, rows), -1, jnp.int32)
        for k in range(3):
            way = d * 3 + k
            for sl in range(slots):
                name = sl if way == 13 else nb[sl, way if way < 13 else way - 1]
                target = jnp.where(key == k * slots + sl, name, target)
        hit = jnp.logical_and(same_z, target == slot)
        sel[d] = jnp.where(hit, 1.0, 0.0).astype(F32).astype(BF16)

    def flip(w, to):
        def body(k, carry):
            to[k] = w[26 - k].astype(F32).T.astype(BF16)
            return carry

        lax.fori_loop(0, 27, body, 0)

    def mask_in(x, carry):
        v = feat[x].astype(F32).reshape(plane, ch) * live[...]
        fld[0, x] = v.astype(BF16).reshape(edge, rows, ch)
        return carry

    lax.fori_loop(0, edge, mask_in, 0)

    pl.semaphore_wait(barrier, n)

    def store(f, x, v):
        fld[f, x] = v.astype(BF16).reshape(edge, rows, ch)

    send(0)
    inner(0, pc_a)
    flip(w2, w2f)
    arrive(0)
    outer(0, pc_a)

    def use1(i, h, v):
        x = 2 * i + h
        pre[x] = v
        store(1, x, v * jax.nn.sigmoid(v) * live[...])

    conv(pc_a, w1, use1)
    send(1)
    inner(1, pc_b)
    flip(w1, w1f)
    arrive(1)
    outer(1, pc_b)

    def use2(i, h, v):
        x = 2 * i + h
        v = v + fld[0, x].reshape(plane, ch).astype(F32)
        s = jax.nn.sigmoid(v)
        out_ref[x] = (v * s * live[...]).astype(BF16).reshape(edge, rows, ch)
        g = cot[x].reshape(plane, ch).astype(F32) * (s * (1.0 + v * (1.0 - s))) * live[...]
        store(2, x, g)
        keep_t(i, h, g)

    conv(pc_b, w2, use2)
    send(2)
    inner(2, pc_c)
    wgrad(pc_b, 0, 0, 3)
    pair_desc(0).start()
    arrive(2)
    outer(2, pc_c)
    scatter(0)

    def use3(i, h, v):
        x = 2 * i + h
        g = v * slope(pre[x]) * live[...]
        store(3, x, g)
        keep_t(i, h, g)

    conv(pc_c, w2f, use3)
    send(3)
    wgrad(pc_a, 1, 0, 2)
    gather(0)
    wgrad(pc_a, 1, 2, 3)
    pair_desc(1).start()
    inner(3, pc_c)
    scatter(1)
    arrive(3)
    outer(3, pc_c)
    forward(0)

    def use4(i, h, v):
        x = 2 * i + h
        g = (fld[2, x].reshape(plane, ch).astype(F32) + v) * live[...]
        gin_ref[x] = g.astype(BF16).reshape(edge, rows, ch)

    conv(pc_c, w1f, use4)
    finish(0, gw2_ref)
    gather(1)
    forward(1)
    finish(1, gw1_ref)
    for f in range(4):
        drain(f)
    drain_sums(0)
    drain_sums(1)


def shards(nx, ny, nd, features, cotangent, first_weight, second_weight, neighbours, counts):
    _, edge, _, slots, _, ch = features.shape
    rows = slots * edge
    plane = edge * rows
    flat = (edge, edge, rows, ch)
    scale = float(nx * ny * nd * slots * edge**3) ** -0.5
    vmem = pl.BlockSpec(memory_space=pltpu.VMEM)
    smem = pl.BlockSpec(memory_space=pltpu.SMEM)
    n = nx * ny
    q = -(-27 * ch // (UNIT * n * nd))
    units = q * n * nd
    gshape = jax.ShapeDtypeStruct((units, UNIT, ch), BF16)
    fshape = jax.ShapeDtypeStruct(flat, BF16)
    out, gin, g1, g2 = pl.pallas_call(
        functools.partial(kernel, nx, ny, nd),
        out_shape=[fshape, fshape, gshape, gshape],
        in_specs=[vmem] * 4 + [smem] * 2,
        out_specs=[vmem] * 4,
        scratch_shapes=[
            pltpu.VMEM((4,) + flat, BF16),
            pltpu.VMEM((4, 2, edge, rows, ch), BF16),
            pltpu.VMEM((4, 2, edge, rows, ch), BF16),
            pltpu.VMEM((4, 4, rows, ch), BF16),
            pltpu.VMEM((edge + 2, edge, rows, 9 * ch), BF16),
            pltpu.VMEM((edge + 2, edge, rows, 9 * ch), BF16),
            pltpu.VMEM((edge + 2, edge, rows, 9 * ch), BF16),
            pltpu.VMEM((edge, plane, ch), F32),
            pltpu.VMEM((2 * ch, edge // 2 * plane), BF16),
            pltpu.SemaphoreType.DMA((4, len(DIRS))),
            pltpu.SemaphoreType.DMA((4, len(DIRS))),
            pltpu.VMEM((27, ch, ch), BF16),
            pltpu.VMEM((27, ch, ch), BF16),
            pltpu.VMEM((9, 3 * rows, rows), BF16),
            pltpu.VMEM((plane, ch), F32),
            pltpu.VMEM((2, units, UNIT, ch), BF16),
            pltpu.VMEM((2, units // nd, UNIT, ch), BF16),
            pltpu.VMEM((2, units // nd, UNIT, ch), BF16),
            pltpu.VMEM((2, n, q, UNIT, ch), BF16),
            pltpu.VMEM((2, units, UNIT, ch), BF16),
        ]
        + [pltpu.SemaphoreType.DMA((2,))] * 2
        + [pltpu.SemaphoreType.DMA((2, n))] * 6,
        compiler_params=pltpu.CompilerParams(
            collective_id=0, has_side_effects=True, vmem_limit_bytes=60 * 1024 * 1024
        ),
    )(
        features.reshape(flat),
        cotangent.reshape(flat),
        first_weight,
        second_weight,
        neighbours[0, 0, 0],
        counts.reshape(1),
    )
    def finish(g):
        g = g.reshape(-1, ch)[: 27 * ch]
        return g.reshape(27, ch, ch).astype(F32) * scale

    return out.reshape(features.shape), gin.reshape(features.shape), finish(g1), finish(g2)


def solution(mesh):
    field = P("dp", "sx", "sy", None, None, None)
    return jax.shard_map(
        functools.partial(shards, mesh.shape["sx"], mesh.shape["sy"], mesh.shape["dp"]),
        mesh=mesh,
        in_specs=(field, field, P(), P(), P("dp", "sx", "sy", None, None), P("dp", "sx", "sy")),
        out_specs=(field, field, P(), P()),
        check_vma=False,
    )
```
